32 devices in a mesh: dp: 2 (over y), expert: 16 (over z, x, core).
Axes of the slice: x: 2, y: 2, z: 4, core: 2. Of those that a mesh axis runs over, the one named last changes fastest.
Arguments:
- soft_tokens: bfloat16 [2048, 2048], P('expert', 'dp'), may hold values from -6 to 6
- expert_ids: int32 [2048, 8], P('expert'), may hold values from 0 to 31, all different within a row; in each aligned block of 128 rows (0 to 127, 128 to 255, ...) at most 40 rows name the same one
- gate_mix: float32 [2048, 8], P('expert'), may hold values from 0.05 to 0.35
- w_gate: bfloat16 [32, 2048, 768], P('expert', 'dp'), may hold values from -0.125 to 0.125
- w_up: bfloat16 [32, 2048, 768], P('expert', 'dp'), may hold values from -0.125 to 0.125
- w_down: bfloat16 [32, 768, 2048], P('expert', None, 'dp'), may hold values from -0.21875 to 0.21875
- out_grad: bfloat16 [2048, 2048], P('expert', 'dp'), may hold values from -6 to 6
Outputs:
- mixed: bfloat16 [2048, 2048], P('expert', 'dp')
- token_grad: bfloat16 [2048, 2048], P('expert', 'dp')
The draws below stay inside these ranges and needn't reach their ends.
Inputs may be any that keep to these rules, and one draw needn't show every extreme that they name: `expert_ids`: each row names 8 different experts. Among the 128 rows of one device no expert is named by more than 40 rows, and in some device one expert is named by exactly 40 rows.
All inputs are finite; a program needn't handle non-finite values.
Results may differ from the reference program's by a relative error of at most 0.023.
Values may be sent and summed in bfloat16 or wider, within the bound.
A program may use at most 128 MiB of HBM per device.

```python
import math
import jax
import jax.numpy as jnp
import numpy as np
from jax import lax

D = 2048
F = 768
TOPK = 8
TOK_DEV = 128
EXPERTS = 32
TOKENS = 2048
CAP = 40
N_DP = 2
N_EXPERT = 16


def block_scale(key, shape, pieces, least, high):
    def one(position, blocks):
        heights = jax.random.uniform(jax.random.fold_in(jax.random.fold_in(key, 6), position), (blocks,), jnp.float32, least / len(pieces), high / len(pieces))
        return jnp.repeat(jnp.exp(heights), shape[position] // blocks).reshape((-1,) + (1,) * (len(shape) - position - 1))

    gain = one(*pieces[0])
    for cut in pieces[1:]:
        gain = gain * one(*cut)
    return gain


def assign_block(stream_key, own, number, rows, count, top, most, slope):
    order = jax.random.permutation(stream_key, count)
    crowded, ordinary = load_shares(count, rows * top, most, slope, True), load_shares(count, rows * top, most, slope, False)
    places = jnp.arange(count)

    def named(lengths, offset_by):
        used = int((lengths > 0).sum())
        fixed = max(1, used // 4)
        passed = fixed + (places - fixed + offset_by * (used - fixed)) % max(1, count - fixed)
        return jnp.zeros((count,), jnp.int32).at[order[jnp.where(places < fixed, places, passed)]].set(jnp.asarray(lengths, jnp.int32))

    lengths = jnp.where(number % 4 == 0, named(crowded, number // 4), named(ordinary, number - number // 4 - 1))
    mixed = jax.random.permutation(jax.random.fold_in(own, 3), count)
    giver, sink = mixed[0:count // 2 * 2:2], mixed[1:count // 2 * 2:2]
    slack = jnp.minimum(lengths[giver] - 1, most - lengths[sink]) // 2
    slack = jnp.where((giver == order[0]) | (sink == order[0]) | (lengths[sink] == 0), 0, jnp.maximum(slack, 0))
    passed = jax.random.randint(jax.random.fold_in(own, 4), (count // 2,), 0, 1 << 20) % (slack + 1)
    lengths = lengths.at[giver].add(-passed).at[sink].add(passed)
    members = jnp.searchsorted(jnp.cumsum(lengths), jnp.arange(rows * top), side="right").astype(jnp.int32)
    table = members.reshape(top, rows).T
    table = table[jax.random.permutation(jax.random.fold_in(own, 1), rows)]
    offset_by = jax.random.randint(jax.random.fold_in(own, 2), (rows, 1), 0, top)
    return jnp.take_along_axis(table, (jnp.arange(top)[None, :] + offset_by) % top, axis=1)


def load_shares(count, total, limit, lean, full):
    loads = [(1 << 20) // math.isqrt(rank ** lean) + 1 for rank in range(1, count + 1)]
    largest = limit if full else min(limit, max(-(-total // count), total * loads[0] // sum(loads)))
    least = 1 if total - largest >= count - 1 else 0
    holding, surplus = [largest] + [least] * (count - 1), total - largest - least * (count - 1)
    while surplus > 0:
        free = [i for i in range(1, count) if holding[i] < largest] or [i for i in range(1, count) if holding[i] < limit]
        whole, remaining = sum([loads[i] for i in free]), surplus
        for i in free:
            addition = min(limit - holding[i], max(1, remaining * loads[i] // whole), surplus)
            holding[i] = holding[i] + addition
            surplus = surplus - addition
    return np.array(holding)


def scatter_about(stream_key, shape, spread, reach, shards=(), held_as=jnp.bfloat16):
    entries = spread * jax.random.normal(stream_key, shape, jnp.float32)
    if shards:
        entries = entries * block_scale(stream_key, shape, shards, -0.22, 0.18)
    return jnp.clip(entries, -reach, reach).astype(held_as)


def setup_inputs(seed: int = 0) -> dict:
    seeds = jax.random.split(jax.random.key(seed), 8)
    soft_tokens = scatter_about(seeds[0], (TOKENS, D), 1.0, 6.0, ((0, 16), (1, 2)))
    expert_ids_keys = jax.random.split(jax.random.fold_in(seeds[1], 1), TOKENS // TOK_DEV)
    expert_ids_turns = jax.random.permutation(jax.random.fold_in(seeds[1], 3), TOKENS // TOK_DEV)
    expert_ids = jax.vmap(lambda own, number: assign_block(jax.random.fold_in(seeds[1], 2), own, number, TOK_DEV, EXPERTS, TOPK, CAP, 2))(expert_ids_keys, expert_ids_turns).reshape((TOKENS, TOPK))
    gate_mix = jnp.clip(0.05 + 0.29999999 * jax.random.uniform(seeds[2], (TOKENS, TOPK), jnp.float32) ** block_scale(seeds[2], (TOKENS, TOPK), ((0, 16),), -0.2, 0.2), 0.05, 0.35)
    w_gate = scatter_about(seeds[3], (EXPERTS, D, F), D ** -0.5, 0.125, ((0, 16), (1, 2)))
    w_up = scatter_about(seeds[4], (EXPERTS, D, F), D ** -0.5, 0.125, ((0, 16), (1, 2)))
    w_down = scatter_about(seeds[5], (EXPERTS, F, D), F ** -0.5, 0.21875, ((0, 16), (2, 2)))
    out_grad = scatter_about(seeds[6], (TOKENS, D), 1.0, 6.0, ((0, 16), (1, 2)))
    return dict(soft_tokens=soft_tokens, expert_ids=expert_ids, gate_mix=gate_mix, w_gate=w_gate, w_up=w_up, w_down=w_down, out_grad=out_grad)


def activate(sums, hidden):
    gate_part = sums[:, :hidden]
    upper_part = sums[:, hidden:]
    sigmoid_gate = jax.nn.sigmoid(gate_part)
    return (gate_part * sigmoid_gate * upper_part).astype(jnp.bfloat16)

def act_grad(sums, back, hidden):
    gate_part = sums[:, :hidden]
    upper_part = sums[:, hidden:]
    sigmoid_gate = jax.nn.sigmoid(gate_part)
    d_gate = back * upper_part * sigmoid_gate * (1.0 + gate_part * (1.0 - sigmoid_gate))
    d_upper = back * gate_part * sigmoid_gate
    return jnp.concatenate([d_gate, d_upper], axis=1).astype(jnp.bfloat16)

def block_sum(rows, weight):
    width_part = D // N_DP
    total = jnp.zeros((rows.shape[0], weight.shape[1]), jnp.float32)
    for part in range(N_DP):
        term = jnp.dot(rows[:, part * width_part:(part + 1) * width_part], weight[part * width_part:(part + 1) * width_part], preferred_element_type=jnp.float32).astype(jnp.bfloat16)
        total = total + lax.optimization_barrier(term).astype(jnp.float32)
    return total

def reference(soft_tokens, expert_ids, gate_mix, w_gate, w_up, w_down, out_grad):
    flat_count = TOKENS * TOPK
    slots = N_EXPERT * CAP
    block_ids = expert_ids.reshape(N_EXPERT, TOK_DEV * TOPK)
    onehot = (block_ids[:, :, None] == jnp.arange(EXPERTS, dtype=jnp.int32)[None, None, :]).astype(jnp.int32)
    before = lax.optimization_barrier(jnp.sum(jnp.cumsum(onehot, axis=1) * onehot, axis=2)) - 1
    column = jnp.arange(N_EXPERT, dtype=jnp.int32)[:, None] * CAP + before
    table = jnp.full((EXPERTS, slots), flat_count, jnp.int32)
    table = table.at[block_ids, column].set(jnp.arange(flat_count, dtype=jnp.int32).reshape(N_EXPERT, TOK_DEV * TOPK))
    w_both = jnp.concatenate([w_gate, w_up], axis=2)
    flat_mix = gate_mix.reshape(flat_count)

    def one_expert(carry, index):
        mixed, grad_in = carry
        entry = table[index]
        valid = entry < flat_count
        token = jnp.minimum(entry // TOPK, TOKENS - 1).astype(jnp.int32)
        weight = jnp.where(valid, flat_mix[jnp.minimum(entry, flat_count - 1)], 0.0)
        rows = jnp.where(valid[:, None], soft_tokens[token], jnp.zeros((), soft_tokens.dtype))
        grads = jnp.where(valid[:, None], out_grad[token], jnp.zeros((), out_grad.dtype))
        both = w_both[index]
        down = w_down[index]
        sums = block_sum(rows, both)
        hidden = activate(sums, F)
        expert_out = jnp.dot(hidden, down, preferred_element_type=jnp.float32).astype(jnp.bfloat16)
        back = block_sum(grads, down.T)
        dpre = act_grad(sums, back, F)
        grad_rows = jnp.dot(dpre, both.T, preferred_element_type=jnp.float32).astype(jnp.bfloat16)
        mixed = mixed.at[token].add(weight[:, None] * expert_out.astype(jnp.float32))
        grad_in = grad_in.at[token].add(weight[:, None] * grad_rows.astype(jnp.float32))
        return ((mixed, grad_in), None)
    start = (jnp.zeros((TOKENS, D), jnp.float32), jnp.zeros((TOKENS, D), jnp.float32))
    (mixed, grad_in), unused = lax.scan(one_expert, start, jnp.arange(EXPERTS, dtype=jnp.int32))
    return (mixed.astype(jnp.bfloat16), grad_in.astype(jnp.bfloat16))
```

```python
import jax
import jax.numpy as jnp
from jax import lax
from jax.sharding import PartitionSpec as P

F32 = jnp.float32
BF16 = jnp.bfloat16


def slot_maps(ids, mix, first, local_experts, capacity):
    tok_rows = ids.shape[1]
    own = first + jnp.arange(local_experts, dtype=jnp.int32)
    hit = ids[:, None, :, :] == own[None, :, None, None]
    named = jnp.any(hit, axis=3)
    weight = jnp.sum(jnp.where(hit, mix[:, None, :, :], 0.0), axis=3)
    before = jnp.arange(tok_rows)[:, None] < jnp.arange(tok_rows)[None, :]
    place = jnp.einsum(
        "set,tu->seu", named.astype(BF16), before.astype(BF16), preferred_element_type=F32
    ).astype(jnp.int32)
    slots = jnp.arange(capacity, dtype=jnp.int32)
    pick = (place[:, :, None, :] == slots[None, None, :, None]) & named[:, :, None, :]
    slot_weight = jnp.sum(jnp.where(pick, weight[:, :, None, :], 0.0), axis=3)
    return pick.astype(BF16), slot_weight


def per_device(soft_tokens, expert_ids, gate_mix, w_gate, w_up, w_down, out_grad):
    tok_rows, width_part = soft_tokens.shape
    top_count = expert_ids.shape[1]
    local_experts = w_gate.shape[0]
    hidden = w_gate.shape[2]
    groups = lax.axis_size("expert")
    dp_count = lax.axis_size("dp")
    experts = groups * local_experts
    capacity = max(2, tok_rows * top_count * 5 // (4 * experts))
    both = lax.all_gather(jnp.concatenate([soft_tokens, out_grad], axis=1), "expert")
    ids = lax.all_gather(expert_ids, "expert")
    mix = lax.all_gather(gate_mix, "expert")
    first = lax.axis_index("expert") * local_experts
    pick, slot_weight = slot_maps(ids, mix, first, local_experts, capacity)
    rows = jnp.einsum("sect,std->secd", pick, both, preferred_element_type=F32).astype(BF16)
    pre = [
        jnp.einsum("secd,edf->secf", rows[..., :width_part], w, preferred_element_type=F32)
        for w in (w_gate, w_up)
    ]
    back = jnp.einsum("secd,efd->secf", rows[..., width_part:], w_down, preferred_element_type=F32)
    part = jnp.concatenate(pre + [back], axis=-1).astype(BF16)
    total = part.astype(F32)
    moved = part
    for _ in range(dp_count - 1):
        moved = lax.ppermute(moved, "dp", [(i, (i + 1) % dp_count) for i in range(dp_count)])
        total = total + moved.astype(F32)
    a = total[..., :hidden]
    b = total[..., hidden : 2 * hidden]
    back = total[..., 2 * hidden :] * slot_weight[..., None]
    sig = jax.nn.sigmoid(a)
    act = (a * sig * b * slot_weight[..., None]).astype(BF16)
    d_gate = (back * b * sig * (1.0 + a * (1.0 - sig))).astype(BF16)
    d_up = (back * a * sig).astype(BF16)
    out = jnp.einsum("secf,efd->secd", act, w_down, preferred_element_type=F32)
    grad = jnp.einsum("secf,edf->secd", d_gate, w_gate, preferred_element_type=F32) + jnp.einsum(
        "secf,edf->secd", d_up, w_up, preferred_element_type=F32
    )
    result = jnp.concatenate([out, grad], axis=-1).astype(BF16)
    spread = jnp.einsum("sect,secd->std", pick, result, preferred_element_type=F32).astype(BF16)
    summed = lax.psum_scatter(spread, "expert", scatter_dimension=0, tiled=False)
    return summed[:, :width_part], summed[:, width_part:]


def solution(mesh):
    in_specs = (
        P("expert", "dp"),
        P("expert", None),
        P("expert", None),
        P("expert", "dp", None),
        P("expert", "dp", None),
        P("expert", None, "dp"),
        P("expert", "dp"),
    )
    out_specs = (P("expert", "dp"), P("expert", "dp"))
    return jax.shard_map(
        per_device, mesh=mesh, in_specs=in_specs, out_specs=out_specs, check_vma=False
    )
```

```python
import functools

import jax
import jax.numpy as jnp
from jax import lax
from jax.experimental import pallas as pl
from jax.experimental.pallas import tpu as pltpu
from jax.sharding import PartitionSpec as P

F32 = jnp.float32
BF16 = jnp.bfloat16


def slot_maps(ids, mix, first, local_experts, capacity):
    tok_rows = ids.shape[1]
    own = first + jnp.arange(local_experts, dtype=jnp.int32)
    hit = ids[:, None, :, :] == own[None, :, None, None]
    named = jnp.any(hit, axis=3)
    weight = jnp.sum(jnp.where(hit, mix[:, None, :, :], 0.0), axis=3)
    before = jnp.arange(tok_rows)[:, None] < jnp.arange(tok_rows)[None, :]
    place = jnp.einsum(
        "set,tu->seu", named.astype(BF16), before.astype(BF16), preferred_element_type=F32
    ).astype(jnp.int32)
    slots = jnp.arange(capacity, dtype=jnp.int32)
    pick = (place[:, :, None, :] == slots[None, None, :, None]) & named[:, :, None, :]
    slot_weight = jnp.sum(jnp.where(pick, weight[:, :, None, :], 0.0), axis=3)
    return pick.astype(BF16), slot_weight


def per_device(soft_tokens, expert_ids, gate_mix, w_gate, w_up, w_down, out_grad):
    tok_rows, width_part = soft_tokens.shape
    top_count = expert_ids.shape[1]
    local_experts = w_gate.shape[0]
    hidden = w_gate.shape[2]
    groups = lax.axis_size("expert")
    dp_count = lax.axis_size("dp")
    experts = groups * local_experts
    capacity = max(2, tok_rows * top_count * 5 // (4 * experts))
    both = lax.all_gather(jnp.concatenate([soft_tokens, out_grad], axis=1), "expert")
    ids = lax.all_gather(expert_ids, "expert")
    mix = lax.all_gather(gate_mix, "expert")
    first = lax.axis_index("expert") * local_experts
    pick, slot_weight = slot_maps(ids, mix, first, local_experts, capacity)
    rows = jnp.einsum("sect,std->secd", pick, both, preferred_element_type=F32).astype(BF16)
    pre = [
        jnp.einsum("secd,edf->secf", rows[..., :width_part], w, preferred_element_type=F32)
        for w in (w_gate, w_up)
    ]
    back = jnp.einsum("secd,efd->secf", rows[..., width_part:], w_down, preferred_element_type=F32)
    part = jnp.concatenate(pre + [back], axis=-1).astype(BF16)
    total = part.astype(F32)
    moved = part
    for _ in range(dp_count - 1):
        moved = lax.ppermute(moved, "dp", [(i, (i + 1) % dp_count) for i in range(dp_count)])
        total = total + moved.astype(F32)
    a = total[..., :hidden]
    b = total[..., hidden : 2 * hidden]
    back = total[..., 2 * hidden :] * slot_weight[..., None]
    sig = jax.nn.sigmoid(a)
    act = (a * sig * b * slot_weight[..., None]).astype(BF16)
    d_gate = (back * b * sig * (1.0 + a * (1.0 - sig))).astype(BF16)
    d_up = (back * a * sig).astype(BF16)
    out = jnp.einsum("secf,efd->secd", act, w_down, preferred_element_type=F32)
    grad = jnp.einsum("secf,edf->secd", d_gate, w_gate, preferred_element_type=F32) + jnp.einsum(
        "secf,edf->secd", d_up, w_up, preferred_element_type=F32
    )
    result = jnp.concatenate([out, grad], axis=-1).astype(BF16)
    spread = jnp.einsum("sect,secd->std", pick, result, preferred_element_type=F32).astype(BF16)
    summed = lax.psum_scatter(spread, "expert", scatter_dimension=0, tiled=False)
    return summed[:, :width_part], summed[:, width_part:]


MESH = pl.DeviceIdType.MESH
MID = 2
CORES = 2


def flip(value, step, count):
    out, bit = 0, 1
    while bit < count:
        out = out + lax.rem(lax.div(value, bit) + lax.div(step, bit), 2) * bit
        bit *= 2
    return out


def fused_kernel(
    groups, x_ref, meta_ref, wg_ref, wu_ref, wd_ref, mixed_ref, tgrad_ref,
    ag, metas, psend, precv, acc, crecv, xsend, xrecv, zsend, zrecv,
    ms, mr, zs, zr, xs, xr, cs, cr, ys, yr, rcs, rcr, rxs, rxr, rzs, rzr,
):
    rows, wide = x_ref.shape
    half = wide // 2
    experts, _, hid = wg_ref.shape
    plane = MID * CORES
    outer = groups // plane
    slots = psend.shape[1] // experts
    me = lax.axis_index("expert")
    y = lax.axis_index("dp")
    z = lax.div(me, plane)
    x = lax.rem(lax.div(me, CORES), MID)
    c = lax.rem(me, CORES)
    core_peer = (z * MID + x) * CORES + 1 - c
    x_peer = (z * MID + 1 - x) * CORES + c

    def at(expert):
        return {"dp": y, "expert": expert}

    def copy(src, dst, send, recv, device):
        return pltpu.make_async_remote_copy(
            src_ref=src, dst_ref=dst, send_sem=send, recv_sem=recv,
            device_id=device, device_id_type=MESH,
        )

    barrier = pltpu.get_barrier_semaphore()
    for k in range(1, groups):
        pl.semaphore_signal(
            barrier, inc=1, device_id=at(lax.rem(me + k, groups)), device_id_type=MESH
        )
    other_dp = {"dp": 1 - y, "expert": me}
    pl.semaphore_signal(barrier, inc=1, device_id=other_dp, device_id_type=MESH)
    pl.semaphore_wait(barrier, groups)

    def meta_copy(k):
        to = lax.rem(me + k, groups)
        return copy(meta_ref.at[to], metas.at[me], ms.at[k], mr.at[k], at(to))

    def meta_arrival(k):
        source = lax.rem(me + groups - k, groups)
        return copy(meta_ref.at[source], metas.at[source], ms.at[k], mr.at[k], at(source))

    def peer_of(step):
        return (flip(z, step, outer) * MID + x) * CORES + c

    def z_copy(step):
        return copy(x_ref, ag.at[me], zs.at[step], zr.at[step], at(peer_of(step)))

    def z_arrival(step):
        blk = peer_of(step)
        return copy(x_ref, ag.at[blk], zs.at[step], zr.at[step], at(blk))

    def x_copy(step, blk):
        return copy(ag.at[blk], ag.at[blk], xs.at[step], xr.at[step], at(x_peer))

    def c_copy(step, which, blk):
        return copy(
            ag.at[blk], ag.at[blk], cs.at[step, which], cr.at[step, which], at(core_peer)
        )

    def y_copy(step):
        return copy(psend.at[step], precv.at[step], ys.at[step], yr.at[step], other_dp)

    def rc_copy(step, across):
        return copy(
            acc.at[across * CORES + 1 - c], crecv.at[step, across],
            rcs.at[step, across], rcr.at[step, across], at(core_peer),
        )

    def rx_copy(step):
        return copy(xsend, xrecv.at[step], rxs.at[step], rxr.at[step], at(x_peer))

    def rz_copy(step):
        return copy(zsend.at[step], zrecv.at[step], rzs.at[step], rzr.at[step], at(peer_of(step)))

    ag[me] = x_ref[...]
    metas[me] = meta_ref[me]
    for k in range(1, groups):
        meta_copy(k).start()
    for i in range(1, outer):
        z_copy(outer - i).start()

    def dot(a, b, dims):
        return lax.dot_general(a, b, (dims, ((), ())), preferred_element_type=jnp.float32)

    def pick_of(p):
        tiles = metas[pl.ds(p * plane, plane)]
        line = jnp.concatenate([tiles[b] for b in range(plane)], axis=1)
        slot = lax.broadcasted_iota(jnp.int32, (slots, plane * rows), 0).astype(jnp.float32)
        picks, weights = [], []
        for e in range(experts):
            match = slot == line[e : e + 1]
            picks.append(jnp.where(match, 1.0, 0.0))
            weights.append(
                jnp.sum(
                    jnp.where(match, line[experts + e : experts + e + 1], 0.0),
                    axis=1, keepdims=True,
                )
            )
        return jnp.concatenate(picks, axis=0), weights

    def first_half(i):
        step = lax.rem(outer - i, outer)
        p = flip(z, step, outer)
        mine = (p * MID + x) * CORES + c
        across = (p * MID + 1 - x) * CORES + c

        @pl.when(i > 0)
        def _():
            z_arrival(step).wait_recv()

        x_copy(step, mine).start()
        c_copy(step, 0, mine).start()

        @pl.when(i == 0)
        def _():
            @pl.loop(1, groups)
            def _(k):
                meta_arrival(k).wait_recv()

        x_copy(step, across).wait_recv()
        c_copy(step, 1, across).start()
        c_copy(step, 0, mine + 1 - 2 * c).wait_recv()
        c_copy(step, 1, across + 1 - 2 * c).wait_recv()
        pick, _ = pick_of(p)
        pick = pick.astype(BF16)
        block = ag[pl.ds(p * plane, plane)].reshape(plane * rows, wide)
        got = dot(pick, block, ((1,), (0,))).astype(BF16)
        for e in range(experts):
            tok = got[e * slots : (e + 1) * slots, :half]
            cot = got[e * slots : (e + 1) * slots, half:]
            span = pl.ds(e * slots, slots)
            psend[step, span, :hid] = dot(tok, wg_ref[e], ((1,), (0,))).astype(BF16)
            psend[step, span, hid : 2 * hid] = dot(tok, wu_ref[e], ((1,), (0,))).astype(BF16)
            psend[step, span, 2 * hid :] = dot(cot, wd_ref[e], ((1,), (1,))).astype(BF16)
        y_copy(step).start()

    def second_half(i):
        step = lax.rem(outer - i, outer)
        p = flip(z, step, outer)
        pick, weights = pick_of(p)
        spread_by = pick.T.astype(BF16)
        y_copy(step).wait_recv()
        outs, grads = [], []
        for e in range(experts):
            span = pl.ds(e * slots, slots)

            def total(lo):
                part = psend[step, span, lo : lo + hid].astype(F32)
                return part + precv[step, span, lo : lo + hid].astype(F32)

            a, b = total(0), total(hid)
            back = total(2 * hid) * weights[e]
            sig = jax.nn.sigmoid(a)
            silu = a * sig
            act = (silu * b * weights[e]).astype(BF16)
            d_gate = (back * b * sig * (1.0 + a * (1.0 - sig))).astype(BF16)
            d_up = (back * silu).astype(BF16)
            outs.append(dot(act, wd_ref[e], ((1,), (0,))).astype(BF16))
            grads.append(
                (
                    dot(d_gate, wg_ref[e], ((1,), (1,))) + dot(d_up, wu_ref[e], ((1,), (1,)))
                ).astype(BF16)
            )
        for lo, part in ((0, outs), (half, grads)):
            rows_out = dot(spread_by, jnp.concatenate(part, axis=0), ((1,), (0,)))
            acc[:, :, lo : lo + half] = rows_out.astype(BF16).reshape(plane, rows, half)
        for m in range(MID):
            rc_copy(step, m).start()
        for m in range(MID):
            rc_copy(step, m).wait_recv()
        there = acc[(1 - x) * CORES + c].astype(F32) + crecv[step, 1 - x].astype(F32)
        xsend[...] = there.astype(BF16)
        rx_copy(step).start()
        here = acc[x * CORES + c].astype(F32) + crecv[step, x].astype(F32)
        rx_copy(step).wait_recv()
        here = (here + xrecv[step].astype(F32)).astype(BF16)

        @pl.when(i == 0)
        def _():
            zrecv[0] = here

        @pl.when(i > 0)
        def _():
            zsend[step] = here
            rz_copy(step).start()

        rx_copy(step).wait_send()
        for m in range(MID):
            rc_copy(step, m).wait_send()

    @pl.loop(0, outer + 1)
    def _(i):
        @pl.when(i < outer)
        def _():
            first_half(i)

        @pl.when(i > 0)
        def _():
            second_half(i - 1)

    @pl.loop(1, groups)
    def _(k):
        meta_copy(k).wait_send()

    for step in range(outer):
        x_copy(step, me).wait_send()
        c_copy(step, 0, me).wait_send()
        c_copy(step, 1, me).wait_send()
        y_copy(step).wait_send()
    for step in range(1, outer):
        z_copy(step).wait_send()
    final = zrecv[0].astype(F32)
    for step in range(1, outer):
        rz_copy(step).wait_recv()
        final = final + zrecv[step].astype(F32)
    for step in range(1, outer):
        rz_copy(step).wait_send()
    mixed_ref[...] = final[:, :half].astype(BF16)
    tgrad_ref[...] = final[:, half:].astype(BF16)


def fused_device(soft_tokens, expert_ids, gate_mix, w_gate, w_up, w_down, out_grad):
    tok_rows, width_part = soft_tokens.shape
    top_count = expert_ids.shape[1]
    local_experts, _, hid = w_gate.shape
    groups = lax.axis_size("expert")
    experts = groups * local_experts
    capacity = max(2, tok_rows * top_count * 5 // (4 * experts))
    plane = MID * CORES
    outer = groups // plane
    wide = 2 * width_part
    ids, mix = expert_ids.T, gate_mix.T
    hit = ids[None] == jnp.arange(experts, dtype=jnp.int32)[:, None, None]
    named = jnp.any(hit, axis=1)
    weight = jnp.sum(jnp.where(hit, mix[None], 0.0), axis=1)
    before = jnp.arange(tok_rows)[:, None] < jnp.arange(tok_rows)[None, :]
    place = jnp.dot(named.astype(BF16), before.astype(BF16), preferred_element_type=F32)
    offset = (lax.axis_index("expert") % plane * capacity).astype(F32)
    key = jnp.where(named, place + offset, -1.0)
    shape = (groups, local_experts, tok_rows)
    meta = jnp.concatenate([key.reshape(shape), weight.reshape(shape)], axis=1)
    meta = jnp.pad(meta, ((0, 0), (0, -2 * local_experts % 8), (0, 0)))
    both = jnp.concatenate([soft_tokens, out_grad], axis=1)
    picked = local_experts * plane * capacity
    vmem = pl.BlockSpec(memory_space=pltpu.VMEM)
    dma = pltpu.SemaphoreType.DMA
    out = jax.ShapeDtypeStruct((tok_rows, width_part), BF16)
    return pl.pallas_call(
        functools.partial(fused_kernel, groups),
        out_shape=(out, out),
        in_specs=[vmem] * 5,
        out_specs=(vmem, vmem),
        scratch_shapes=[
            pltpu.VMEM((groups, tok_rows, wide), BF16),
            pltpu.VMEM(meta.shape, F32),
            pltpu.VMEM((outer, picked, 3 * hid), BF16),
            pltpu.VMEM((outer, picked, 3 * hid), BF16),
            pltpu.VMEM((plane, tok_rows, wide), BF16),
            pltpu.VMEM((outer, MID, tok_rows, wide), BF16),
            pltpu.VMEM((tok_rows, wide), BF16),
            pltpu.VMEM((outer, tok_rows, wide), BF16),
            pltpu.VMEM((outer, tok_rows, wide), BF16),
            pltpu.VMEM((outer, tok_rows, wide), BF16),
            dma((groups,)), dma((groups,)),
            dma((outer,)), dma((outer,)),
            dma((outer,)), dma((outer,)),
            dma((outer, MID)), dma((outer, MID)),
            dma((outer,)), dma((outer,)),
            dma((outer, MID)), dma((outer, MID)),
            dma((outer,)), dma((outer,)),
            dma((outer,)), dma((outer,)),
        ],
        compiler_params=pltpu.CompilerParams(
            collective_id=0, has_side_effects=True, vmem_limit_bytes=67043328
        ),
    )(both, meta, w_gate, w_up, w_down)


def solution(mesh):
    in_specs = (
        P("expert", "dp"),
        P("expert", None),
        P("expert", None),
        P("expert", "dp", None),
        P("expert", "dp", None),
        P("expert", None, "dp"),
        P("expert", "dp"),
    )
    out_specs = (P("expert", "dp"), P("expert", "dp"))
    fits = mesh.shape["dp"] == 2 and mesh.shape["expert"] in (4, 8, 16)
    return jax.shard_map(
        fused_device if fits else per_device,
        mesh=mesh, in_specs=in_specs, out_specs=out_specs, check_vma=False,
    )
```

```python
import functools

import jax
import jax.numpy as jnp
from jax import lax
from jax.experimental import pallas as pl
from jax.experimental.pallas import tpu as pltpu
from jax.sharding import PartitionSpec as P

F32 = jnp.float32
BF16 = jnp.bfloat16


def slot_maps(ids, mix, first, local_experts, capacity):
    tok_rows = ids.shape[1]
    own = first + jnp.arange(local_experts, dtype=jnp.int32)
    hit = ids[:, None, :, :] == own[None, :, None, None]
    named = jnp.any(hit, axis=3)
    weight = jnp.sum(jnp.where(hit, mix[:, None, :, :], 0.0), axis=3)
    before = jnp.arange(tok_rows)[:, None] < jnp.arange(tok_rows)[None, :]
    place = jnp.einsum(
        "set,tu->seu", named.astype(BF16), before.astype(BF16), preferred_element_type=F32
    ).astype(jnp.int32)
    slots = jnp.arange(capacity, dtype=jnp.int32)
    pick = (place[:, :, None, :] == slots[None, None, :, None]) & named[:, :, None, :]
    slot_weight = jnp.sum(jnp.where(pick, weight[:, :, None, :], 0.0), axis=3)
    return pick.astype(BF16), slot_weight


def per_device(soft_tokens, expert_ids, gate_mix, w_gate, w_up, w_down, out_grad):
    tok_rows, width_part = soft_tokens.shape
    top_count = expert_ids.shape[1]
    local_experts = w_gate.shape[0]
    hidden = w_gate.shape[2]
    groups = lax.axis_size("expert")
    dp_count = lax.axis_size("dp")
    experts = groups * local_experts
    capacity = max(2, tok_rows * top_count * 5 // (4 * experts))
    both = lax.all_gather(jnp.concatenate([soft_tokens, out_grad], axis=1), "expert")
    ids = lax.all_gather(expert_ids, "expert")
    mix = lax.all_gather(gate_mix, "expert")
    first = lax.axis_index("expert") * local_experts
    pick, slot_weight = slot_maps(ids, mix, first, local_experts, capacity)
    rows = jnp.einsum("sect,std->secd", pick, both, preferred_element_type=F32).astype(BF16)
    pre = [
        jnp.einsum("secd,edf->secf", rows[..., :width_part], w, preferred_element_type=F32)
        for w in (w_gate, w_up)
    ]
    back = jnp.einsum("secd,efd->secf", rows[..., width_part:], w_down, preferred_element_type=F32)
    part = jnp.concatenate(pre + [back], axis=-1).astype(BF16)
    total = part.astype(F32)
    moved = part
    for _ in range(dp_count - 1):
        moved = lax.ppermute(moved, "dp", [(i, (i + 1) % dp_count) for i in range(dp_count)])
        total = total + moved.astype(F32)
    a = total[..., :hidden]
    b = total[..., hidden : 2 * hidden]
    back = total[..., 2 * hidden :] * slot_weight[..., None]
    sig = jax.nn.sigmoid(a)
    act = (a * sig * b * slot_weight[..., None]).astype(BF16)
    d_gate = (back * b * sig * (1.0 + a * (1.0 - sig))).astype(BF16)
    d_up = (back * a * sig).astype(BF16)
    out = jnp.einsum("secf,efd->secd", act, w_down, preferred_element_type=F32)
    grad = jnp.einsum("secf,edf->secd", d_gate, w_gate, preferred_element_type=F32) + jnp.einsum(
        "secf,edf->secd", d_up, w_up, preferred_element_type=F32
    )
    result = jnp.concatenate([out, grad], axis=-1).astype(BF16)
    spread = jnp.einsum("sect,secd->std", pick, result, preferred_element_type=F32).astype(BF16)
    summed = lax.psum_scatter(spread, "expert", scatter_dimension=0, tiled=False)
    return summed[:, :width_part], summed[:, width_part:]


MESH = pl.DeviceIdType.MESH
MID = 2
CORES = 2


def flip(value, step, count):
    out, bit = 0, 1
    while bit < count:
        out = out + lax.rem(lax.div(value, bit) + lax.div(step, bit), 2) * bit
        bit *= 2
    return out


def fused_kernel(
    groups, x_ref, meta_ref, wg_ref, wu_ref, wd_ref, mixed_ref, tgrad_ref,
    ag, metas, psend, precv, acc, crecv, xsend, xrecv, zsend, zrecv,
    ms, mr, zs, zr, xs, xr, cs, cr, ys, yr, rcs, rcr, rxs, rxr, rzs, rzr,
):
    rows, wide = x_ref.shape
    half = wide // 2
    experts, _, hid = wg_ref.shape
    plane = MID * CORES
    outer = groups // plane
    slots = psend.shape[2]
    me = lax.axis_index("expert")
    y = lax.axis_index("dp")
    z = lax.div(me, plane)
    x = lax.rem(lax.div(me, CORES), MID)
    c = lax.rem(me, CORES)
    core_peer = (z * MID + x) * CORES + 1 - c
    x_peer = (z * MID + 1 - x) * CORES + c

    def at(expert):
        return {"dp": y, "expert": expert}

    def copy(src, dst, send, recv, device):
        return pltpu.make_async_remote_copy(
            src_ref=src, dst_ref=dst, send_sem=send, recv_sem=recv,
            device_id=device, device_id_type=MESH,
        )

    barrier = pltpu.get_barrier_semaphore()
    for k in range(1, groups):
        pl.semaphore_signal(
            barrier, inc=1, device_id=at(lax.rem(me + k, groups)), device_id_type=MESH
        )
    other_dp = {"dp": 1 - y, "expert": me}
    pl.semaphore_signal(barrier, inc=1, device_id=other_dp, device_id_type=MESH)
    pl.semaphore_wait(barrier, groups)

    def meta_copy(k):
        to = lax.rem(me + k, groups)
        return copy(meta_ref.at[to], metas.at[me], ms.at[k], mr.at[k], at(to))

    def meta_arrival(k):
        source = lax.rem(me + groups - k, groups)
        return copy(meta_ref.at[source], metas.at[source], ms.at[k], mr.at[k], at(source))

    def peer_of(step):
        return (flip(z, step, outer) * MID + x) * CORES + c

    def z_copy(step):
        return copy(x_ref, ag.at[me], zs.at[step], zr.at[step], at(peer_of(step)))

    def z_arrival(step):
        blk = peer_of(step)
        return copy(x_ref, ag.at[blk], zs.at[step], zr.at[step], at(blk))

    def x_copy(step, blk):
        return copy(ag.at[blk], ag.at[blk], xs.at[step], xr.at[step], at(x_peer))

    def c_copy(step, which, blk):
        return copy(
            ag.at[blk], ag.at[blk], cs.at[step, which], cr.at[step, which], at(core_peer)
        )

    def y_copy(step, e):
        return copy(
            psend.at[step, e], precv.at[step, e], ys.at[step, e], yr.at[step, e], other_dp
        )

    def rc_copy(step, part, across):
        return copy(
            acc.at[part, across * CORES + 1 - c], crecv.at[step, part, across],
            rcs.at[step, part, across], rcr.at[step, part, across], at(core_peer),
        )

    def rx_copy(step, part):
        return copy(
            xsend.at[part], xrecv.at[step, part],
            rxs.at[step, part], rxr.at[step, part], at(x_peer),
        )

    def rz_copy(step, part):
        return copy(
            zsend.at[step, part], zrecv.at[step, part],
            rzs.at[step, part], rzr.at[step, part], at(peer_of(step)),
        )

    ag[me] = x_ref[...]
    metas[me] = meta_ref[me]
    for k in range(1, groups):
        meta_copy(k).start()
    for i in range(1, outer):
        z_copy(outer - i).start()

    def dot(a, b, dims):
        return lax.dot_general(a, b, (dims, ((), ())), preferred_element_type=jnp.float32)

    def pick_of(p):
        tiles = metas[pl.ds(p * plane, plane)]
        line = jnp.concatenate([tiles[b] for b in range(plane)], axis=1)
        slot = lax.broadcasted_iota(jnp.int32, (slots, plane * rows), 0).astype(jnp.float32)
        picks, weights = [], []
        for e in range(experts):
            match = slot == line[e : e + 1]
            picks.append(jnp.where(match, 1.0, 0.0))
            weights.append(
                jnp.sum(
                    jnp.where(match, line[experts + e : experts + e + 1], 0.0),
                    axis=1, keepdims=True,
                )
            )
        return jnp.concatenate(picks, axis=0), weights

    def first_half(i):
        step = lax.rem(outer - i, outer)
        p = flip(z, step, outer)
        mine = (p * MID + x) * CORES + c
        across = (p * MID + 1 - x) * CORES + c

        @pl.when(i > 0)
        def _():
            z_arrival(step).wait_recv()

        x_copy(step, mine).start()
        c_copy(step, 0, mine).start()

        @pl.when(i == 0)
        def _():
            @pl.loop(1, groups)
            def _(k):
                meta_arrival(k).wait_recv()

        x_copy(step, across).wait_recv()
        c_copy(step, 1, across).start()
        c_copy(step, 0, mine + 1 - 2 * c).wait_recv()
        c_copy(step, 1, across + 1 - 2 * c).wait_recv()
        pick, _ = pick_of(p)
        pick = pick.astype(BF16)
        block = ag[pl.ds(p * plane, plane)].reshape(plane * rows, wide)
        for e in range(experts):
            got = dot(pick[e * slots : (e + 1) * slots], block, ((1,), (0,))).astype(BF16)
            tok, cot = got[:, :half], got[:, half:]
            psend[step, e, :, :hid] = dot(tok, wg_ref[e], ((1,), (0,))).astype(BF16)
            psend[step, e, :, hid : 2 * hid] = dot(tok, wu_ref[e], ((1,), (0,))).astype(BF16)
            psend[step, e, :, 2 * hid :] = dot(cot, wd_ref[e], ((1,), (1,))).astype(BF16)
            y_copy(step, e).start()

    def second_half(i):
        step = lax.rem(outer - i, outer)
        p = flip(z, step, outer)
        pick, weights = pick_of(p)
        spread_by = pick.T.astype(BF16)
        outs, changes = [], []
        for e in range(experts):
            y_copy(step, e).wait_recv()

            def total(lo):
                part = psend[step, e, :, lo : lo + hid].astype(F32)
                return part + precv[step, e, :, lo : lo + hid].astype(F32)

            a, b = total(0), total(hid)
            back = total(2 * hid) * weights[e]
            sig = jax.nn.sigmoid(a)
            silu = a * sig
            act = (silu * b * weights[e]).astype(BF16)
            d_gate = (back * b * sig * (1.0 + a * (1.0 - sig))).astype(BF16)
            changes.append((d_gate, (back * silu).astype(BF16)))
            outs.append(dot(act, wd_ref[e], ((1,), (0,))).astype(BF16))

        def scatter(part, values):
            rows_out = dot(spread_by, jnp.concatenate(values, axis=0), ((1,), (0,)))
            acc[part] = rows_out.astype(BF16).reshape(plane, rows, half)
            for m in range(MID):
                rc_copy(step, part, m).start()

        scatter(0, outs)
        grads = [
            (
                dot(changes[e][0], wg_ref[e], ((1,), (1,)))
                + dot(changes[e][1], wu_ref[e], ((1,), (1,)))
            ).astype(BF16)
            for e in range(experts)
        ]

        def to_x_peer(part):
            for m in range(MID):
                rc_copy(step, part, m).wait_recv()
            there = acc[part, (1 - x) * CORES + c].astype(F32)
            xsend[part] = (there + crecv[step, part, 1 - x].astype(F32)).astype(BF16)
            rx_copy(step, part).start()

        def to_owner(part):
            here = acc[part, x * CORES + c].astype(F32) + crecv[step, part, x].astype(F32)
            rx_copy(step, part).wait_recv()
            here = (here + xrecv[step, part].astype(F32)).astype(BF16)

            @pl.when(i == 0)
            def _():
                zrecv[0, part] = here

            @pl.when(i > 0)
            def _():
                zsend[step, part] = here
                rz_copy(step, part).start()

        to_x_peer(0)
        scatter(1, grads)
        to_x_peer(1)
        to_owner(0)
        to_owner(1)
        for part in range(2):
            rx_copy(step, part).wait_send()
            for m in range(MID):
                rc_copy(step, part, m).wait_send()

    ahead = 2

    @pl.loop(0, outer + ahead)
    def _(i):
        @pl.when(i < outer)
        def _():
            first_half(i)

        @pl.when(i >= ahead)
        def _():
            second_half(i - ahead)

    @pl.loop(1, groups)
    def _(k):
        meta_copy(k).wait_send()

    for step in range(outer):
        x_copy(step, me).wait_send()
        c_copy(step, 0, me).wait_send()
        c_copy(step, 1, me).wait_send()
        for e in range(experts):
            y_copy(step, e).wait_send()
    for step in range(1, outer):
        z_copy(step).wait_send()
    for part, out_ref in enumerate((mixed_ref, tgrad_ref)):
        final = zrecv[0, part].astype(F32)
        for step in range(1, outer):
            rz_copy(step, part).wait_recv()
            final = final + zrecv[step, part].astype(F32)
        out_ref[...] = final.astype(BF16)
    for step in range(1, outer):
        for part in range(2):
            rz_copy(step, part).wait_send()


def fused_device(soft_tokens, expert_ids, gate_mix, w_gate, w_up, w_down, out_grad):
    tok_rows, width_part = soft_tokens.shape
    top_count = expert_ids.shape[1]
    local_experts, _, hid = w_gate.shape
    groups = lax.axis_size("expert")
    experts = groups * local_experts
    capacity = max(2, tok_rows * top_count * 5 // (4 * experts))
    plane = MID * CORES
    outer = groups // plane
    wide = 2 * width_part
    ids, mix = expert_ids.T, gate_mix.T
    hit = ids[None] == jnp.arange(experts, dtype=jnp.int32)[:, None, None]
    named = jnp.any(hit, axis=1)
    weight = jnp.sum(jnp.where(hit, mix[None], 0.0), axis=1)
    before = jnp.arange(tok_rows)[:, None] < jnp.arange(tok_rows)[None, :]
    place = jnp.dot(named.astype(BF16), before.astype(BF16), preferred_element_type=F32)
    offset = (lax.axis_index("expert") % plane * capacity).astype(F32)
    key = jnp.where(named, place + offset, -1.0)
    shape = (groups, local_experts, tok_rows)
    meta = jnp.concatenate([key.reshape(shape), weight.reshape(shape)], axis=1)
    meta = jnp.pad(meta, ((0, 0), (0, -2 * local_experts % 8), (0, 0)))
    both = jnp.concatenate([soft_tokens, out_grad], axis=1)
    slots = plane * capacity
    vmem = pl.BlockSpec(memory_space=pltpu.VMEM)
    dma = pltpu.SemaphoreType.DMA
    out = jax.ShapeDtypeStruct((tok_rows, width_part), BF16)
    return pl.pallas_call(
        functools.partial(fused_kernel, groups),
        out_shape=(out, out),
        in_specs=[vmem] * 5,
        out_specs=(vmem, vmem),
        scratch_shapes=[
            pltpu.VMEM((groups, tok_rows, wide), BF16),
            pltpu.VMEM(meta.shape, F32),
            pltpu.VMEM((outer, local_experts, slots, 3 * hid), BF16),
            pltpu.VMEM((outer, local_experts, slots, 3 * hid), BF16),
            pltpu.VMEM((2, plane, tok_rows, width_part), BF16),
            pltpu.VMEM((outer, 2, MID, tok_rows, width_part), BF16),
            pltpu.VMEM((2, tok_rows, width_part), BF16),
            pltpu.VMEM((outer, 2, tok_rows, width_part), BF16),
            pltpu.VMEM((outer, 2, tok_rows, width_part), BF16),
            pltpu.VMEM((outer, 2, tok_rows, width_part), BF16),
            dma((groups,)), dma((groups,)),
            dma((outer,)), dma((outer,)),
            dma((outer,)), dma((outer,)),
            dma((outer, MID)), dma((outer, MID)),
            dma((outer, local_experts)), dma((outer, local_experts)),
            dma((outer, 2, MID)), dma((outer, 2, MID)),
            dma((outer, 2)), dma((outer, 2)),
            dma((outer, 2)), dma((outer, 2)),
        ],
        compiler_params=pltpu.CompilerParams(
            collective_id=0, has_side_effects=True, vmem_limit_bytes=67043328
        ),
    )(both, meta, w_gate, w_up, w_down)


def solution(mesh):
    in_specs = (
        P("expert", "dp"),
        P("expert", None),
        P("expert", None),
        P("expert", "dp", None),
        P("expert", "dp", None),
        P("expert", None, "dp"),
        P("expert", "dp"),
    )
    out_specs = (P("expert", "dp"), P("expert", "dp"))
    fits = mesh.shape["dp"] == 2 and mesh.shape["expert"] in (4, 8, 16)
    return jax.shard_map(
        fused_device if fits else per_device,
        mesh=mesh, in_specs=in_specs, out_specs=out_specs, check_vma=False,
    )
```

```python
import functools

import jax
import jax.numpy as jnp
from jax import lax
from jax.experimental import pallas as pl
from jax.experimental.pallas import tpu as pltpu
from jax.sharding import PartitionSpec as P

F32 = jnp.float32
BF16 = jnp.bfloat16


def slot_maps(ids, mix, first, local_experts, capacity):
    tok_rows = ids.shape[1]
    own = first + jnp.arange(local_experts, dtype=jnp.int32)
    hit = ids[:, None, :, :] == own[None, :, None, None]
    named = jnp.any(hit, axis=3)
    weight = jnp.sum(jnp.where(hit, mix[:, None, :, :], 0.0), axis=3)
    before = jnp.arange(tok_rows)[:, None] < jnp.arange(tok_rows)[None, :]
    place = jnp.einsum(
        "set,tu->seu", named.astype(BF16), before.astype(BF16), preferred_element_type=F32
    ).astype(jnp.int32)
    slots = jnp.arange(capacity, dtype=jnp.int32)
    pick = (place[:, :, None, :] == slots[None, None, :, None]) & named[:, :, None, :]
    slot_weight = jnp.sum(jnp.where(pick, weight[:, :, None, :], 0.0), axis=3)
    return pick.astype(BF16), slot_weight


def per_device(soft_tokens, expert_ids, gate_mix, w_gate, w_up, w_down, out_grad):
    tok_rows, width_part = soft_tokens.shape
    top_count = expert_ids.shape[1]
    local_experts = w_gate.shape[0]
    hidden = w_gate.shape[2]
    groups = lax.axis_size("expert")
    dp_count = lax.axis_size("dp")
    experts = groups * local_experts
    capacity = max(2, tok_rows * top_count * 5 // (4 * experts))
    both = lax.all_gather(jnp.concatenate([soft_tokens, out_grad], axis=1), "expert")
    ids = lax.all_gather(expert_ids, "expert")
    mix = lax.all_gather(gate_mix, "expert")
    first = lax.axis_index("expert") * local_experts
    pick, slot_weight = slot_maps(ids, mix, first, local_experts, capacity)
    rows = jnp.einsum("sect,std->secd", pick, both, preferred_element_type=F32).astype(BF16)
    pre = [
        jnp.einsum("secd,edf->secf", rows[..., :width_part], w, preferred_element_type=F32)
        for w in (w_gate, w_up)
    ]
    back = jnp.einsum("secd,efd->secf", rows[..., width_part:], w_down, preferred_element_type=F32)
    part = jnp.concatenate(pre + [back], axis=-1).astype(BF16)
    total = part.astype(F32)
    moved = part
    for _ in range(dp_count - 1):
        moved = lax.ppermute(moved, "dp", [(i, (i + 1) % dp_count) for i in range(dp_count)])
        total = total + moved.astype(F32)
    a = total[..., :hidden]
    b = total[..., hidden : 2 * hidden]
    back = total[..., 2 * hidden :] * slot_weight[..., None]
    sig = jax.nn.sigmoid(a)
    act = (a * sig * b * slot_weight[..., None]).astype(BF16)
    d_gate = (back * b * sig * (1.0 + a * (1.0 - sig))).astype(BF16)
    d_up = (back * a * sig).astype(BF16)
    out = jnp.einsum("secf,efd->secd", act, w_down, preferred_element_type=F32)
    grad = jnp.einsum("secf,edf->secd", d_gate, w_gate, preferred_element_type=F32) + jnp.einsum(
        "secf,edf->secd", d_up, w_up, preferred_element_type=F32
    )
    result = jnp.concatenate([out, grad], axis=-1).astype(BF16)
    spread = jnp.einsum("sect,secd->std", pick, result, preferred_element_type=F32).astype(BF16)
    summed = lax.psum_scatter(spread, "expert", scatter_dimension=0, tiled=False)
    return summed[:, :width_part], summed[:, width_part:]


MESH = pl.DeviceIdType.MESH
MID = 2
CORES = 2


def flip(value, step, count):
    out, bit = 0, 1
    while bit < count:
        out = out + lax.rem(lax.div(value, bit) + lax.div(step, bit), 2) * bit
        bit *= 2
    return out


def fused_kernel(
    groups, x_ref, meta_ref, wg_ref, wu_ref, wd_ref, mixed_ref, tgrad_ref,
    ag, metas, psend, precv, acc, crecv, xsend, xrecv, zsend, zrecv,
    ms, mr, zs, zr, xs, xr, cs, cr, ys, yr, rcs, rcr, rxs, rxr, rzs, rzr,
):
    rows, wide = x_ref.shape
    half = wide // 2
    experts, _, hid = wg_ref.shape
    plane = MID * CORES
    outer = groups // plane
    slots = psend.shape[2]
    me = lax.axis_index("expert")
    y = lax.axis_index("dp")
    z = lax.div(me, plane)
    x = lax.rem(lax.div(me, CORES), MID)
    c = lax.rem(me, CORES)
    core_peer = (z * MID + x) * CORES + 1 - c
    x_peer = (z * MID + 1 - x) * CORES + c

    def at(expert):
        return {"dp": y, "expert": expert}

    def copy(src, dst, send, recv, device):
        return pltpu.make_async_remote_copy(
            src_ref=src, dst_ref=dst, send_sem=send, recv_sem=recv,
            device_id=device, device_id_type=MESH,
        )

    barrier = pltpu.get_barrier_semaphore()
    for k in range(1, groups):
        pl.semaphore_signal(
            barrier, inc=1, device_id=at(lax.rem(me + k, groups)), device_id_type=MESH
        )
    other_dp = {"dp": 1 - y, "expert": me}
    pl.semaphore_signal(barrier, inc=1, device_id=other_dp, device_id_type=MESH)
    pl.semaphore_wait(barrier, groups)

    def meta_copy(k):
        to = lax.rem(me + k, groups)
        return copy(meta_ref.at[to], metas.at[me], ms.at[k], mr.at[k], at(to))

    def meta_arrival(k):
        source = lax.rem(me + groups - k, groups)
        return copy(meta_ref.at[source], metas.at[source], ms.at[k], mr.at[k], at(source))

    def peer_of(step):
        return (flip(z, step, outer) * MID + x) * CORES + c

    def z_copy(step):
        return copy(x_ref, ag.at[me], zs.at[step], zr.at[step], at(peer_of(step)))

    def z_arrival(step):
        blk = peer_of(step)
        return copy(x_ref, ag.at[blk], zs.at[step], zr.at[step], at(blk))

    def x_copy(step, blk):
        return copy(ag.at[blk], ag.at[blk], xs.at[step], xr.at[step], at(x_peer))

    def c_copy(step, which, blk):
        return copy(
            ag.at[blk], ag.at[blk], cs.at[step, which], cr.at[step, which], at(core_peer)
        )

    def y_copy(step, e):
        return copy(
            psend.at[step, e], precv.at[step, e], ys.at[step, e], yr.at[step, e], other_dp
        )

    def rc_copy(step, part, across):
        return copy(
            acc.at[part, across * CORES + 1 - c], crecv.at[step, part, across],
            rcs.at[step, part, across], rcr.at[step, part, across], at(core_peer),
        )

    def rx_copy(step, part):
        return copy(
            xsend.at[part], xrecv.at[step, part],
            rxs.at[step, part], rxr.at[step, part], at(x_peer),
        )

    def rz_copy(step, part):
        return copy(
            zsend.at[step, part], zrecv.at[step, part],
            rzs.at[step, part], rzr.at[step, part], at(peer_of(step)),
        )

    ag[me] = x_ref[...]
    metas[me] = meta_ref[me]
    for k in range(1, groups):
        meta_copy(k).start()
    for i in range(1, outer):
        z_copy(outer - i).start()

    def dot(a, b, dims):
        return lax.dot_general(a, b, (dims, ((), ())), preferred_element_type=jnp.float32)

    def pick_of(p):
        tiles = metas[pl.ds(p * plane, plane)]
        line = jnp.concatenate([tiles[b] for b in range(plane)], axis=1)
        slot = lax.broadcasted_iota(jnp.int32, (slots, plane * rows), 0).astype(jnp.float32)
        picks, weights = [], []
        for e in range(experts):
            match = slot == line[e : e + 1]
            picks.append(jnp.where(match, 1.0, 0.0))
            weights.append(
                jnp.sum(
                    jnp.where(match, line[experts + e : experts + e + 1], 0.0),
                    axis=1, keepdims=True,
                )
            )
        return jnp.concatenate(picks, axis=0), weights

    def first_half(i):
        step = lax.rem(outer - i, outer)
        p = flip(z, step, outer)
        mine = (p * MID + x) * CORES + c
        across = (p * MID + 1 - x) * CORES + c

        @pl.when(i > 0)
        def _():
            z_arrival(step).wait_recv()

        x_copy(step, mine).start()
        c_copy(step, 0, mine).start()

        @pl.when(i == 0)
        def _():
            @pl.loop(1, groups)
            def _(k):
                meta_arrival(k).wait_recv()

        x_copy(step, across).wait_recv()
        c_copy(step, 1, across).start()
        c_copy(step, 0, mine + 1 - 2 * c).wait_recv()
        c_copy(step, 1, across + 1 - 2 * c).wait_recv()
        pick, _ = pick_of(p)
        pick = pick.astype(BF16)
        block = ag[pl.ds(p * plane, plane)].reshape(plane * rows, wide)
        for e in range(experts):
            got = dot(pick[e * slots : (e + 1) * slots], block, ((1,), (0,))).astype(BF16)
            tok, cot = got[:, :half], got[:, half:]
            psend[step, e, :, :hid] = dot(tok, wg_ref[e], ((1,), (0,))).astype(BF16)
            psend[step, e, :, hid : 2 * hid] = dot(tok, wu_ref[e], ((1,), (0,))).astype(BF16)
            psend[step, e, :, 2 * hid :] = dot(cot, wd_ref[e], ((1,), (1,))).astype(BF16)
            y_copy(step, e).start()

    def second_half(i):
        step = lax.rem(outer - i, outer)
        p = flip(z, step, outer)
        pick, weights = pick_of(p)
        spread_by = pick.T.astype(BF16)
        outs, changes, grads = [], [], []

        def grad_of(e):
            by_gate = dot(changes[e][0], wg_ref[e], ((1,), (1,)))
            return (by_gate + dot(changes[e][1], wu_ref[e], ((1,), (1,)))).astype(BF16)

        for e in range(experts):
            y_copy(step, e).wait_recv()

            def total(lo):
                part = psend[step, e, :, lo : lo + hid].astype(F32)
                return part + precv[step, e, :, lo : lo + hid].astype(F32)

            a, b = total(0), total(hid)
            back = total(2 * hid) * weights[e]
            sig = jax.nn.sigmoid(a)
            silu = a * sig
            act = (silu * b * weights[e]).astype(BF16)
            d_gate = (back * b * sig * (1.0 + a * (1.0 - sig))).astype(BF16)
            changes.append((d_gate, (back * silu).astype(BF16)))
            outs.append(dot(act, wd_ref[e], ((1,), (0,))).astype(BF16))
            if e < experts - 1:
                grads.append(grad_of(e))

        def scatter(part, values):
            rows_out = dot(spread_by, jnp.concatenate(values, axis=0), ((1,), (0,)))
            acc[part] = rows_out.astype(BF16).reshape(plane, rows, half)
            for m in range(MID):
                rc_copy(step, part, m).start()

        scatter(0, outs)
        grads.append(grad_of(experts - 1))

        def to_x_peer(part):
            for m in range(MID):
                rc_copy(step, part, m).wait_recv()
            there = acc[part, (1 - x) * CORES + c].astype(F32)
            xsend[part] = (there + crecv[step, part, 1 - x].astype(F32)).astype(BF16)
            rx_copy(step, part).start()

        def to_owner(part):
            here = acc[part, x * CORES + c].astype(F32) + crecv[step, part, x].astype(F32)
            rx_copy(step, part).wait_recv()
            here = (here + xrecv[step, part].astype(F32)).astype(BF16)

            @pl.when(i == 0)
            def _():
                zrecv[0, part] = here

            @pl.when(i > 0)
            def _():
                zsend[step, part] = here
                rz_copy(step, part).start()

        to_x_peer(0)
        scatter(1, grads)
        to_x_peer(1)
        to_owner(0)
        to_owner(1)
        for part in range(2):
            rx_copy(step, part).wait_send()
            for m in range(MID):
                rc_copy(step, part, m).wait_send()

    ahead = max(1, outer - 1)

    @pl.loop(0, outer + ahead)
    def _(i):
        @pl.when(i < outer)
        def _():
            first_half(i)

        @pl.when(i >= ahead)
        def _():
            second_half(i - ahead)

    @pl.loop(1, groups)
    def _(k):
        meta_copy(k).wait_send()

    for step in range(outer):
        x_copy(step, me).wait_send()
        c_copy(step, 0, me).wait_send()
        c_copy(step, 1, me).wait_send()
        for e in range(experts):
            y_copy(step, e).wait_send()
    for step in range(1, outer):
        z_copy(step).wait_send()
    for part, out_ref in enumerate((mixed_ref, tgrad_ref)):
        final = zrecv[0, part].astype(F32)
        for step in range(1, outer):
            rz_copy(step, part).wait_recv()
            final = final + zrecv[step, part].astype(F32)
        out_ref[...] = final.astype(BF16)
    for step in range(1, outer):
        for part in range(2):
            rz_copy(step, part).wait_send()


def fused_device(soft_tokens, expert_ids, gate_mix, w_gate, w_up, w_down, out_grad):
    tok_rows, width_part = soft_tokens.shape
    top_count = expert_ids.shape[1]
    local_experts, _, hid = w_gate.shape
    groups = lax.axis_size("expert")
    experts = groups * local_experts
    capacity = max(2, tok_rows * top_count * 5 // (4 * experts))
    plane = MID * CORES
    outer = groups // plane
    wide = 2 * width_part
    ids, mix = expert_ids.T, gate_mix.T
    hit = ids[None] == jnp.arange(experts, dtype=jnp.int32)[:, None, None]
    named = jnp.any(hit, axis=1)
    weight = jnp.sum(jnp.where(hit, mix[None], 0.0), axis=1)
    before = jnp.arange(tok_rows)[:, None] < jnp.arange(tok_rows)[None, :]
    place = jnp.dot(named.astype(BF16), before.astype(BF16), preferred_element_type=F32)
    offset = (lax.axis_index("expert") % plane * capacity).astype(F32)
    key = jnp.where(named, place + offset, -1.0)
    shape = (groups, local_experts, tok_rows)
    meta = jnp.concatenate([key.reshape(shape), weight.reshape(shape)], axis=1)
    meta = jnp.pad(meta, ((0, 0), (0, -2 * local_experts % 8), (0, 0)))
    both = jnp.concatenate([soft_tokens, out_grad], axis=1)
    slots = plane * capacity
    vmem = pl.BlockSpec(memory_space=pltpu.VMEM)
    dma = pltpu.SemaphoreType.DMA
    out = jax.ShapeDtypeStruct((tok_rows, width_part), BF16)
    return pl.pallas_call(
        functools.partial(fused_kernel, groups),
        out_shape=(out, out),
        in_specs=[vmem] * 5,
        out_specs=(vmem, vmem),
        scratch_shapes=[
            pltpu.VMEM((groups, tok_rows, wide), BF16),
            pltpu.VMEM(meta.shape, F32),
            pltpu.VMEM((outer, local_experts, slots, 3 * hid), BF16),
            pltpu.VMEM((outer, local_experts, slots, 3 * hid), BF16),
            pltpu.VMEM((2, plane, tok_rows, width_part), BF16),
            pltpu.VMEM((outer, 2, MID, tok_rows, width_part), BF16),
            pltpu.VMEM((2, tok_rows, width_part), BF16),
            pltpu.VMEM((outer, 2, tok_rows, width_part), BF16),
            pltpu.VMEM((outer, 2, tok_rows, width_part), BF16),
            pltpu.VMEM((outer, 2, tok_rows, width_part), BF16),
            dma((groups,)), dma((groups,)),
            dma((outer,)), dma((outer,)),
            dma((outer,)), dma((outer,)),
            dma((outer, MID)), dma((outer, MID)),
            dma((outer, local_experts)), dma((outer, local_experts)),
            dma((outer, 2, MID)), dma((outer, 2, MID)),
            dma((outer, 2)), dma((outer, 2)),
            dma((outer, 2)), dma((outer, 2)),
        ],
        compiler_params=pltpu.CompilerParams(
            collective_id=0, has_side_effects=True, vmem_limit_bytes=67043328
        ),
    )(both, meta, w_gate, w_up, w_down)


def solution(mesh):
    in_specs = (
        P("expert", "dp"),
        P("expert", None),
        P("expert", None),
        P("expert", "dp", None),
        P("expert", "dp", None),
        P("expert", None, "dp"),
        P("expert", "dp"),
    )
    out_specs = (P("expert", "dp"), P("expert", "dp"))
    fits = mesh.shape["dp"] == 2 and mesh.shape["expert"] in (4, 8, 16)
    return jax.shard_map(
        fused_device if fits else per_device,
        mesh=mesh, in_specs=in_specs, out_specs=out_specs, check_vma=False,
    )
```
